32 devices in a mesh: snap: 2 (over y), row: 4 (over z), col: 4 (over x, core).
Axes of the slice: x: 2, y: 2, z: 4, core: 2. Of those that a mesh axis runs over, the one named last changes fastest.
Arguments:
- orbitals: float32 [12288, 768], P(('snap', 'row', 'col')), parts along dimension 0, may hold values from -6 to 6
- screened: float32 [6, 6144, 6144], P('snap', 'row', 'col'), parts along dimension 0, may hold values from -0.0029296875 to 0.0029296875
- green_weight: float32 [6, 768], P('snap'), parts along dimension 0, may hold values from 0.05 to 1
- time_weight: float32 [3], replicated, may hold values from 0.3 to 1
Outputs:
- updated: float32 [12288, 768], P(('snap', 'row', 'col')), parts along dimension 0
The draws below stay inside these ranges and needn't reach their ends.
There are 2 independent parts, one for each index of `snap`. The reference program is written for one: setup_inputs(seed, part) draws one part's arguments, and reference() takes and returns one part's arrays. A program takes and returns all parts, laid end to end along the dimension named above; an argument that names none is the same for every part. Nothing has to cross between parts.
All inputs are finite; a program needn't handle non-finite values.
Results may differ from the reference program's by a relative error of at most 0.00013.
Values sent between devices are 32-bit elements; how exact they have to be, the bound alone decides.
A program may use at most 128 MiB of HBM per device.

```python
import math
import jax
import jax.numpy as jnp
from jax import lax

NP = 6144
NORB = 768
TIMES = 3
PASSES = 2


def level_of(stream_key, shape, split, smallest, high):
    gain = 1.0
    for axis_at, parts in split:
        steps = jax.random.uniform(jax.random.fold_in(jax.random.fold_in(stream_key, 6), axis_at), (parts,), jnp.float32, smallest / len(split), high / len(split))
        gain = gain * jnp.repeat(jnp.exp(steps), shape[axis_at] // parts).reshape((-1,) + (1,) * (len(shape) - 1 - axis_at))
    return gain


def centred(key, dims, scale, bound, cuts=(), dtype=jnp.bfloat16):
    array = jax.random.normal(key, dims, jnp.float32) * scale
    if len(cuts) > 0:
        array = level_of(key, dims, cuts, -0.22, 0.18) * array
    return jnp.clip(array, min=-bound, max=bound).astype(dtype)


def setup_inputs(seed: int = 0, part: int = 0) -> dict:
    streams_of = jax.random.split(jax.random.key(seed), 5)
    part_splits = jax.random.split(jax.random.fold_in(streams_of[4], part), 5)
    orbitals = centred(part_splits[0], (NP, NORB), 1.0, 6.0, ((0, 16),), jnp.float32)
    screened = centred(part_splits[1], (TIMES, NP, NP), (NP * NORB) ** -0.5, 0.0029296875, ((1, 4), (2, 4)), jnp.float32)
    green_weight = jnp.clip(jnp.exp(jax.random.uniform(part_splits[2], (TIMES, NORB), jnp.float32, math.log(0.05), math.log(1.0))), 0.05, 1.0)
    time_weight = jnp.clip(jax.random.uniform(streams_of[3], (TIMES,), jnp.float32, 0.3, 1.0), 0.3, 1.0)
    return dict(orbitals=orbitals, screened=screened, green_weight=green_weight, time_weight=time_weight)


def reference(orbitals, screened, green_weight, time_weight):
    phi = orbitals
    for step in range(PASSES):
        correction = jnp.zeros(phi.shape, jnp.float32)
        for t in range(TIMES):
            green = lax.dot_general(phi * green_weight[t], phi, (((1,), (1,)), ((), ())), precision=lax.Precision.HIGHEST, preferred_element_type=jnp.float32)
            applied = jnp.dot(green * screened[t], phi, precision=lax.Precision.HIGHEST, preferred_element_type=jnp.float32)
            correction = correction + time_weight[t] * applied
        phi = phi - correction
    return phi
```

```python
import functools

import jax
import jax.numpy as jnp
from jax import lax
from jax.experimental import pallas as pl
from jax.experimental.pallas import tpu as pltpu
from jax.sharding import PartitionSpec as P

PASSES = 2


def split(value):
    high = value.astype(jnp.bfloat16)
    low = (value - high.astype(jnp.float32)).astype(jnp.bfloat16)
    return high, low


def apply_kernel(times, parts, has_total, index_ref, *refs):
    rows_refs, refs = refs[:parts], refs[parts:]
    cols_refs, refs = refs[:parts], refs[parts:]
    weight_ref, screened_ref, refs = refs[0], refs[1], refs[2:]
    total_refs = None
    if has_total:
        total_refs, refs = refs[:parts], refs[parts:]
    out_refs, (weighted, plain) = refs[:parts], refs[parts:]

    @pl.when(pl.program_id(0) == 0)
    def _():
        cols = jnp.concatenate([ref[...] for ref in cols_refs], axis=1)
        width, depth = cols.shape
        high, low = split(cols)
        plain[0:width, :] = high
        plain[width : 2 * width, :] = high
        plain[2 * width : 3 * width, :] = low
        for t in range(times):
            high, low = split((cols * weight_ref[t : t + 1, :]).T)
            weighted[t, 0:depth, :] = high
            weighted[t, depth : 2 * depth, :] = high
            weighted[t, 2 * depth : 3 * depth, :] = low

    high, low = split(jnp.concatenate([ref[...] for ref in rows_refs], axis=1))
    rows = jnp.concatenate([high, low, high], axis=1)
    mixed = None
    for t in range(times):
        green = jnp.dot(rows, weighted[t], preferred_element_type=jnp.float32)
        term = green * screened_ref[t]
        mixed = term if mixed is None else mixed + term
    high, low = split(mixed)
    mixed = jnp.concatenate([high, low, high], axis=1)
    applied = jnp.dot(mixed, plain[...], preferred_element_type=jnp.float32)
    part = applied.shape[1] // parts
    for k in range(parts):
        value = applied[:, k * part : (k + 1) * part]
        out_refs[k][...] = value + total_refs[k][...] if has_total else value


def apply_block(index, rows, cols, weight, screened, total):
    times = screened.shape[0]
    parts = len(rows)
    n_rows, part = rows[0].shape
    depth = parts * part
    width = cols[0].shape[0]
    tile = next(k for k in (512, 384, 256, 128, n_rows) if n_rows % k == 0)
    row_spec = pl.BlockSpec((tile, part), lambda i, ix: (i, 0))
    in_specs = [row_spec] * parts
    in_specs += [pl.BlockSpec((width, part), lambda i, ix: (0, 0))] * parts
    in_specs += [
        pl.BlockSpec((times, depth), lambda i, ix: (0, 0)),
        pl.BlockSpec((times, tile, width), lambda i, ix: (0, i, ix[0])),
    ]
    args = [index, *rows, *cols, weight, screened]
    if total is not None:
        in_specs += [row_spec] * parts
        args += total
    return pl.pallas_call(
        functools.partial(apply_kernel, times, parts, total is not None),
        out_shape=[jax.ShapeDtypeStruct((n_rows, part), jnp.float32)] * parts,
        grid_spec=pltpu.PrefetchScalarGridSpec(
            num_scalar_prefetch=1,
            grid=(n_rows // tile,),
            in_specs=in_specs,
            out_specs=[row_spec] * parts,
            scratch_shapes=[
                pltpu.VMEM((times, 3 * depth, width), jnp.bfloat16),
                pltpu.VMEM((3 * width, depth), jnp.bfloat16),
            ],
        ),
        compiler_params=pltpu.CompilerParams(
            dimension_semantics=("arbitrary",), vmem_limit_bytes=56 * 1024 * 1024
        ),
        cost_estimate=pl.CostEstimate(
            flops=6 * (times + 1) * n_rows * width * depth,
            bytes_accessed=4 * (times * n_rows * width + 3 * n_rows * depth),
            transcendentals=0,
        ),
    )(*args)


def scatter_rows(value):
    n_col = lax.axis_size("col")
    if n_col & (n_col - 1):
        return lax.psum_scatter(value, "col", scatter_dimension=0, tiled=True)
    me = lax.axis_index("col")
    points = value.shape[0] // n_col
    value = value.reshape(n_col, points, value.shape[1])
    distance = 1
    while distance < n_col:
        bit = (me // distance) % 2
        pairs = value.reshape((value.shape[0] // 2, 2) + value.shape[1:])
        mine = lax.dynamic_index_in_dim(pairs, bit, 1, keepdims=False)
        theirs = lax.dynamic_index_in_dim(pairs, 1 - bit, 1, keepdims=False)
        swap = [(k, k ^ distance) for k in range(n_col)]
        value = mine + lax.ppermute(theirs, "col", swap)
        distance *= 2
    return value[0]


def body(orbitals, screened, green_weight, time_weight):
    n_row = lax.axis_size("row")
    n_col = lax.axis_size("col")
    factor = n_col // n_row
    points, depth = orbitals.shape
    weight = green_weight * time_weight[:, None]
    to_columns = [
        ((c // factor) * n_col + (c % factor) * n_row + m, m * n_col + c)
        for m in range(n_row)
        for c in range(n_col)
    ]
    ring = [(k, (k + 1) % n_row) for k in range(n_row)]
    me = lax.axis_index("row")
    parts = 1
    own = jnp.split(orbitals, parts, axis=1)
    for step in range(PASSES):
        piece = [lax.ppermute(o, ("row", "col"), to_columns) for o in own]
        rows = [lax.all_gather(o, "col", axis=0, tiled=True) for o in own]
        total = None
        if points % 128 == 0:
            for hop in range(n_row):
                later = None
                if hop < n_row - 1:
                    if total is not None:
                        piece, total = lax.optimization_barrier((piece, total))
                    later = [lax.ppermute(p, "row", ring) for p in piece]
                index = lax.rem(me - hop + n_row, n_row).astype(jnp.int32).reshape(1)
                total = apply_block(index, rows, piece, weight, screened, total)
                piece = later
        else:
            columns = [lax.all_gather(p, "row", axis=0, tiled=True) for p in piece]
            index = jnp.zeros((1,), jnp.int32)
            total = apply_block(index, rows, columns, weight, screened, None)
        own = [
            o - scatter_rows(v)
            for o, v in zip(own, total)
        ]
    return jnp.concatenate(own, axis=1)


def solution(mesh):
    in_specs = (P(("snap", "row", "col"), None), P("snap", "row", "col"), P("snap", None), P())
    out_specs = P(("snap", "row", "col"), None)
    return jax.shard_map(body, mesh=mesh, in_specs=in_specs, out_specs=out_specs, check_vma=False)
```
